32 devices in a mesh: groups: 2 (over y), cells: 8 (over z, x), freq: 2 (over core).
Axes of the slice: x: 2, y: 2, z: 4, core: 2. Of those that a mesh axis runs over, the one named last changes fastest.
Arguments:
- adjoint: float32 [2, 256], P(None, ('groups', 'cells')), parts along dimension 1, may hold values from -6 to 6
- target_x: float32 [256], P(('groups', 'cells')), parts along dimension 0, may hold values from 0 to 1024
- target_y: float32 [256], P(('groups', 'cells')), parts along dimension 0, may hold values from 0 to 8
- target_z: float32 [256], P(('groups', 'cells')), parts along dimension 0, may hold values from 256 to 512
- assignment: int32 [256], P(('groups', 'cells')), parts along dimension 0, may hold values from 0 to 63
- level_codes: int32 [16384], P(('groups', 'cells', 'freq')), parts along dimension 0, may hold values from 0 to 15
- cell_params: bfloat16 [8, 16384], P(None, ('groups', 'cells', 'freq')), parts along dimension 1, may hold values from -5 to 5
- level_table: bfloat16 [16, 256], replicated, may hold values from -4 to 4
- w_proj: bfloat16 [8, 256], replicated, may hold values from -2 to 2
- w_one: bfloat16 [256, 256], replicated, may hold values from -0.375 to 0.375
- b_one: float32 [256], replicated, may hold values from -3 to 3
- w_two: bfloat16 [256, 256], replicated, may hold values from -0.375 to 0.375
- b_two: float32 [256], replicated, may hold values from -3 to 3
- w_out: bfloat16 [256, 128], replicated, may hold values from -0.375 to 0.375
Outputs:
- grad_out: float32 [512, 128], P('groups'), parts along dimension 0
- grad_w2: float32 [512, 256], P('groups'), parts along dimension 0
- grad_b2: float32 [512], P('groups'), parts along dimension 0
- grad_w1: float32 [512, 256], P('groups'), parts along dimension 0
- grad_b1: float32 [512], P('groups'), parts along dimension 0
- grad_table: float32 [32, 256], P('groups'), parts along dimension 0
- grad_proj: float32 [16, 256], P('groups'), parts along dimension 0
- grad_params: float32 [8, 16384], P(None, ('groups', 'cells', 'freq')), parts along dimension 1
The draws below stay inside these ranges and needn't reach their ends.
There are 2 independent parts, one for each index of `groups`. The reference program is written for one: setup_inputs(seed, part) draws one part's arguments, and reference() takes and returns one part's arrays. A program takes and returns all parts, laid end to end along the dimension named above; an argument that names none is the same for every part. Nothing has to cross between parts.
All inputs are finite; a program needn't handle non-finite values.
Results may differ from the reference program's by a relative error of at most 0.01.
Values may be sent and summed in bfloat16 or wider, within the bound.
A program may use at most 64 MiB of HBM per device.

```python
import math
import jax
import jax.numpy as jnp
from jax import lax

F = 64
H = 256
LEVELS = 16
NP = 8
SIDE = 1024
CELLS = 8192
TARGETS = 128


def touch_ends(entries, key, smallest, largest):
    extent = entries.shape
    place = [jax.random.randint(jax.random.fold_in(key, axis), (), 0, extent[axis]) for axis in range(len(extent))]
    entries = entries.at[tuple(place)].set(smallest)
    longest = extent.index(max(extent))
    place[longest] = (place[longest] + 1) % extent[longest]
    return entries.at[tuple(place)].set(largest)


def block_levels(stream_key, dims, shards, low, high):
    def one(axis_at, parts):
        draws = jax.random.uniform(jax.random.fold_in(jax.random.fold_in(stream_key, 6), axis_at), (parts,), jnp.float32, low / len(shards), high / len(shards))
        return jnp.repeat(jnp.exp(draws), dims[axis_at] // parts).reshape((-1,) + (1,) * (len(dims) - axis_at - 1))

    factor_of = one(*shards[0])
    for cut in shards[1:]:
        factor_of = factor_of * one(*cut)
    return factor_of


def centred(key, extent, scale, most, pieces=(), kind=jnp.bfloat16):
    result = scale * jax.random.normal(key, extent, jnp.float32)
    if pieces:
        result = result * block_levels(key, extent, pieces, -0.22, 0.18)
    return jnp.clip(result, -most, most).astype(kind)


def setup_inputs(seed: int = 0, part: int = 0) -> dict:
    arg_keys = jax.random.split(jax.random.key(seed), 15)
    own_keys = jax.random.split(jax.random.fold_in(arg_keys[14], part), 15)
    adjoint = centred(own_keys[0], (2, TARGETS), 1.0, 6.0, ((1, 8),), jnp.float32)
    target_x = jnp.clip(1024.0 * jax.random.uniform(own_keys[1], (TARGETS,), jnp.float32) ** block_levels(own_keys[1], (TARGETS,), ((0, 8),), -0.2, 0.2), 0.0, 1024.0)
    target_y = jnp.clip(8.0 * jax.random.uniform(own_keys[2], (TARGETS,), jnp.float32) ** block_levels(own_keys[2], (TARGETS,), ((0, 8),), -0.2, 0.2), 0.0, 8.0)
    target_z = jnp.clip(256.0 + 256.0 * jax.random.uniform(own_keys[3], (TARGETS,), jnp.float32) ** block_levels(own_keys[3], (TARGETS,), ((0, 8),), -0.2, 0.2), 256.0, 512.0)
    assignment = touch_ends(jax.random.randint(own_keys[4], (TARGETS,), 0, F), jax.random.fold_in(own_keys[4], 1), 0, F - 1).astype(jnp.int32)
    level_codes = touch_ends(jax.random.randint(own_keys[5], (CELLS,), 0, LEVELS), jax.random.fold_in(own_keys[5], 1), 0, LEVELS - 1).astype(jnp.int32)
    cell_params = centred(own_keys[6], (NP, CELLS), 1.0, 5.0, ((1, 16),))
    level_table = centred(arg_keys[7], (LEVELS, H), 0.7, 4.0)
    w_proj = centred(arg_keys[8], (NP, H), NP ** -0.5, 2.0)
    w_one = centred(arg_keys[9], (H, H), H ** -0.5, 0.375)
    b_one = centred(arg_keys[10], (H,), 0.5, 3.0, (), jnp.float32)
    w_two = centred(arg_keys[11], (H, H), H ** -0.5, 0.375)
    b_two = centred(arg_keys[12], (H,), 0.5, 3.0, (), jnp.float32)
    w_out = centred(arg_keys[13], (H, 2 * F), H ** -0.5, 0.375)
    return dict(adjoint=adjoint, target_x=target_x, target_y=target_y, target_z=target_z, assignment=assignment, level_codes=level_codes, cell_params=cell_params, level_table=level_table, w_proj=w_proj, w_one=w_one, b_one=b_one, w_two=w_two, b_two=b_two, w_out=w_out)


wave_low = 1.0
wave_high = 3.0
kernel_gain = 150.0

def silu_slope(value):
    sigma = jax.nn.sigmoid(value)
    return sigma * (1.0 + value * (1.0 - sigma))

def contract(left, right, left_dim, right_dim):
    return lax.dot_general(left, right, (((left_dim,), (right_dim,)), ((), ())), preferred_element_type=jnp.float32)

def kernel_tile(point_x, point_y, point_z, freq_value, cell_col, cell_row, count_freq):
    wave = wave_low + (wave_high - wave_low) * freq_value / (count_freq - 1)
    offset_x = point_x[:, None] - cell_col[None, :]
    offset_y = point_y[:, None] - cell_row[None, :]
    square = offset_x * offset_x + offset_y * offset_y + (point_z * point_z)[:, None]
    distance = jnp.sqrt(square)
    amplitude = kernel_gain * point_z[:, None] / square
    phase = wave[:, None] * distance
    return ((amplitude * jnp.cos(phase)).astype(jnp.bfloat16), (amplitude * jnp.sin(phase)).astype(jnp.bfloat16))

def forward_pass(level_codes, cell_params, level_table, w_proj, w_one, b_one, w_two, b_two):
    levels = level_table.shape[0]
    onehot = (level_codes[:, None] == jnp.arange(levels, dtype=jnp.int32)[None, :]).astype(jnp.bfloat16)
    hidden_in = (jnp.dot(onehot, level_table, preferred_element_type=jnp.float32) + contract(cell_params, w_proj, 0, 0)).astype(jnp.bfloat16)
    pre_one = jnp.dot(hidden_in, w_one, preferred_element_type=jnp.float32) + b_one
    act_one = jax.nn.silu(pre_one).astype(jnp.bfloat16)
    pre_two = jnp.dot(act_one, w_two, preferred_element_type=jnp.float32) + b_two
    act_two = jax.nn.silu(pre_two).astype(jnp.bfloat16)
    return (onehot, hidden_in, pre_one, act_one, pre_two, act_two)

def upper_grads(spectra, w_out, act_one, pre_two, act_two):
    back_two = contract(spectra, w_out, 0, 1)
    delta_two = (back_two * silu_slope(pre_two)).astype(jnp.bfloat16)
    grad_out = contract(act_two, spectra, 0, 1)
    grad_w2 = contract(act_one, delta_two, 0, 0)
    grad_b2 = lax.optimization_barrier(jnp.sum(delta_two.astype(jnp.float32), axis=0))
    return ((grad_out, grad_w2, grad_b2), delta_two)

def lower_grads(delta_two, w_two, w_one, pre_one, hidden_in, onehot, cell_params, w_proj):
    back_one = contract(delta_two, w_two, 1, 1)
    delta_one = (back_one * silu_slope(pre_one)).astype(jnp.bfloat16)
    grad_w1 = contract(hidden_in, delta_one, 0, 0)
    grad_b1 = lax.optimization_barrier(jnp.sum(delta_one.astype(jnp.float32), axis=0))
    back_zero = contract(delta_one, w_one, 1, 1).astype(jnp.bfloat16)
    grad_table = contract(onehot, back_zero, 0, 0)
    grad_proj = contract(cell_params, back_zero, 1, 0)
    grad_params = contract(w_proj, back_zero, 1, 1)
    return ((grad_w1, grad_b1, grad_table, grad_proj), grad_params)

def reference(adjoint, target_x, target_y, target_z, assignment, level_codes, cell_params, level_table, w_proj, w_one, b_one, w_two, b_two, w_out):
    adj_round = lax.optimization_barrier(adjoint.astype(jnp.bfloat16)).astype(jnp.float32)
    freq_value = assignment.astype(jnp.float32)
    blocks = CELLS // SIDE
    scale = 1.0 / math.sqrt(CELLS)

    def step(carry, block):
        start = block * SIDE
        index = start + jnp.arange(SIDE, dtype=jnp.int32)
        cell_col = (index % SIDE).astype(jnp.float32)
        cell_row = (index // SIDE).astype(jnp.float32)
        kre, kim = kernel_tile(target_x, target_y, target_z, freq_value, cell_col, cell_row, F)
        kre, kim = lax.optimization_barrier((kre, kim))
        kre = kre.astype(jnp.float32)
        kim = kim.astype(jnp.float32)
        real_part = jax.ops.segment_sum(kre * adj_round[0][:, None] + kim * adj_round[1][:, None], assignment, num_segments=F)
        imag_part = jax.ops.segment_sum(kre * adj_round[1][:, None] - kim * adj_round[0][:, None], assignment, num_segments=F)
        spectra = jnp.concatenate([real_part, imag_part], axis=0).astype(jnp.bfloat16)
        codes_block = lax.dynamic_slice_in_dim(level_codes, start, SIDE)
        params_block = lax.dynamic_slice_in_dim(cell_params, start, SIDE, axis=1)
        onehot, hidden_in, pre_one, act_one, pre_two, act_two = forward_pass(codes_block, params_block, level_table, w_proj, w_one, b_one, w_two, b_two)
        upper, delta_two = upper_grads(spectra, w_out, act_one, pre_two, act_two)
        lower, grad_params = lower_grads(delta_two, w_two, w_one, pre_one, hidden_in, onehot, params_block, w_proj)
        carry = tuple((total + term for total, term in zip(carry, upper + lower)))
        return (carry, grad_params)
    init = (jnp.zeros((H, 2 * F), jnp.float32), jnp.zeros((H, H), jnp.float32), jnp.zeros((H,), jnp.float32), jnp.zeros((H, H), jnp.float32), jnp.zeros((H,), jnp.float32), jnp.zeros((LEVELS, H), jnp.float32), jnp.zeros((NP, H), jnp.float32))
    totals, params_grads = lax.scan(step, init, jnp.arange(blocks, dtype=jnp.int32))
    grad_params = jnp.moveaxis(params_grads, 0, 1).reshape(NP, CELLS)
    return (totals[0] * scale, totals[1] * scale, totals[2] * scale, totals[3] * scale, totals[4] * scale, totals[5] * scale, totals[6] * scale, grad_params)
```

```python
import functools
import math

import jax
import jax.numpy as jnp
from jax import lax
from jax.experimental import pallas as pl
from jax.experimental.pallas import tpu as pltpu
from jax.sharding import PartitionSpec as P

SIDE = 1024
LANES = 128
WIRE = jnp.bfloat16
WIRE_ROWS = 16

wave_low = 1.0
wave_high = 3.0
kernel_gain = 150.0

f32 = jnp.float32
bf16 = jnp.bfloat16


def contract(left, right, left_dim, right_dim):
    return lax.dot_general(
        left, right, (((left_dim,), (right_dim,)), ((), ())), preferred_element_type=f32
    )


def sin_cos(phase):
    turns = jnp.floor(phase * (2.0 / math.pi) + 0.5)
    rest = phase - turns * 1.5703125
    rest = rest - turns * 4.837512969970703125e-4
    rest = rest - turns * 7.54978995489188216e-8
    square = rest * rest
    sine = rest + rest * square * (
        -1.6666654611e-1 + square * (8.3321608736e-3 + square * -1.9515295891e-4)
    )
    cosine = (
        1.0
        - 0.5 * square
        + square
        * square
        * (4.166664568298827e-2 + square * (-1.388731625493765e-3 + square * 2.443315711809948e-5))
    )
    quarter = turns.astype(jnp.int32)
    odd = (quarter & 1) == 1
    sin_part = jnp.where(odd, cosine, sine)
    cos_part = jnp.where(odd, sine, cosine)
    sin_part = jnp.where((quarter & 2) == 2, -sin_part, sin_part)
    cos_part = jnp.where(((quarter + 1) & 2) == 2, -cos_part, cos_part)
    return sin_part, cos_part


def each(count, step):
    if count <= 16:
        for k in range(1, count):
            step(k)
    else:

        @pl.loop(1, count)
        def _(k):
            step(k)


def kernel(
    dims,
    adj_ref,
    x_ref,
    y_ref,
    z_ref,
    asg_ref,
    codes_ref,
    params_ref,
    table_ref,
    proj_ref,
    w1_ref,
    b1_ref,
    w2_ref,
    b2_ref,
    wo_ref,
    go_ref,
    gw2_ref,
    gb2_ref,
    gw1_ref,
    gb1_ref,
    gt_ref,
    gp_ref,
    gc_ref,
    gath,
    feat,
    hid,
    act1,
    slope1,
    act2,
    slope2,
    spec,
    d2,
    d1,
    part_a,
    part_b,
    cs_a,
    cs_b,
    cr_a,
    cr_b,
    rs_a,
    rs_b,
    rr_a,
    rr_b,
    ag_a,
    ag_b,
    g_send,
    g_recv,
    c_send,
    c_recv,
    rs_send_a,
    rs_recv_a,
    rs_send_b,
    rs_recv_b,
    ag_send_a,
    ag_recv_a,
    ag_send_b,
    ag_recv_b,
    fw_send_a,
    fw_recv_a,
    fw_send_b,
    fw_recv_b,
):
    n, nf, per, piece_a, piece_b, scale = dims
    me = lax.axis_index("cells")
    core = lax.axis_index("freq")
    other = 1 - core
    cells = codes_ref.shape[1]
    local = x_ref.shape[1]
    hidden = w1_ref.shape[0]
    half = hidden // nf
    levels = table_ref.shape[0]
    n_par = proj_ref.shape[0]
    outs = wo_ref.shape[1]
    freqs = outs // 2

    def peer(k):
        return {"cells": lax.rem(me + k, n)}

    def source(k):
        return lax.rem(me + n - k, n)

    mate = {"freq": other}

    def remote(src, dst, send, recv, device):
        return pltpu.make_async_remote_copy(
            src_ref=src,
            dst_ref=dst,
            send_sem=send,
            recv_sem=recv,
            device_id=device,
            device_id_type=pl.DeviceIdType.MESH,
        )

    barrier = pltpu.get_barrier_semaphore()
    each(
        n,
        lambda k: pl.semaphore_signal(
            barrier, inc=1, device_id=peer(k), device_id_type=pl.DeviceIdType.MESH
        ),
    )
    pl.semaphore_signal(barrier, inc=1, device_id=mate, device_id_type=pl.DeviceIdType.MESH)

    width = per * local
    rows = jnp.concatenate(
        [
            adj_ref[...],
            x_ref[...],
            y_ref[...],
            z_ref[...],
            asg_ref[...].astype(f32),
            jnp.zeros((2, local), f32),
        ],
        axis=0,
    )
    spread = jnp.concatenate([rows] * per, axis=1)
    lane = lax.broadcasted_iota(jnp.int32, (8, width), 1)
    start = lax.rem(me, per) * local
    inside = jnp.logical_and(lane >= start, lane < start + local)
    gath[me] = jnp.where(inside, spread, 0.0)

    codes = codes_ref[...]
    onehot = (
        jnp.where(codes == lax.broadcasted_iota(jnp.int32, (levels, cells), 0), 1.0, 0.0)
    ).astype(bf16)
    feat[0:levels, :] = onehot
    hid[...] = (
        contract(onehot, table_ref[...], 0, 0) + contract(params_ref[...], proj_ref[...], 0, 0)
    ).astype(bf16)
    pre = contract(hid[...], w1_ref[...], 1, 0) + b1_ref[...]
    sig = 1.0 / (1.0 + jnp.exp(-pre))
    act1[...] = (pre * sig).astype(bf16)
    slope1[...] = sig * (1.0 + pre * (1.0 - sig))

    pl.semaphore_wait(barrier, n)

    def gather_copy(k):
        return remote(gath.at[me], gath.at[me], g_send.at[k], g_recv.at[k], peer(k))

    each(n, lambda k: gather_copy(k).start())

    pre = contract(act1[...], w2_ref[...], 1, 0) + b2_ref[...]
    sig = 1.0 / (1.0 + jnp.exp(-pre))
    act2[...] = (pre * sig).astype(bf16)
    slope2[...] = sig * (1.0 + pre * (1.0 - sig))

    each(n, lambda k: gather_copy(k).wait())

    index = (me * nf + core) * cells + lax.broadcasted_iota(jnp.int32, (cells, width), 0)
    cell_col = (index % SIDE).astype(f32)
    cell_row = (index // SIDE).astype(f32)
    line = lax.broadcasted_iota(jnp.int32, (outs, width), 0)
    upper = line < freqs
    freq_line = jnp.where(upper, line, line - freqs).astype(f32)

    def section(first):
        block = gath[first]
        for j in range(1, per):
            block = block + gath[first + j]
        adj = block[0:2].astype(bf16).astype(f32)
        a0, a1 = adj[0:1], adj[1:2]
        px, py, pz, pf = block[2:3], block[3:4], block[4:5], block[5:6]
        wave = wave_low + (wave_high - wave_low) * pf / (freqs - 1)
        off_x = px - cell_col
        off_y = py - cell_row
        square = off_x * off_x + off_y * off_y + pz * pz
        distance = jnp.sqrt(square)
        amplitude = (kernel_gain * pz) / square
        sine, cosine = sin_cos(wave * distance)
        kre = (amplitude * cosine).astype(bf16)
        kim = (amplitude * sine).astype(bf16)
        chosen = freq_line == pf
        left_re = jnp.where(chosen, jnp.where(upper, a0, a1), 0.0).astype(bf16)
        left_im = jnp.where(chosen, jnp.where(upper, a1, -a0), 0.0).astype(bf16)
        return contract(kre, left_re, 1, 1) + contract(kim, left_im, 1, 1)

    if n == per:
        total = section(0)
    else:
        total = lax.fori_loop(
            0,
            n // per,
            lambda i, acc: acc + section(i * per),
            jnp.zeros((cells, outs), f32),
        )
    spec[...] = total.astype(bf16)

    delta2 = (contract(spec[...], wo_ref[...], 1, 1) * slope2[...]).astype(bf16)
    d2[...] = delta2
    grad_b2 = jnp.sum(delta2.astype(f32), axis=0, keepdims=True)
    grad = contract(act2[...], spec[...], 0, 0)
    for c in range(nf):
        part_a[c, 0:half, :] = grad[c * half : (c + 1) * half]
    grad = contract(act1[...], d2[...], 0, 0)
    for c in range(nf):
        part_a[c, half : half + hidden, :] = grad[:, c * half : (c + 1) * half]
    used_a = half + hidden
    if used_a < n * piece_a:
        part_a[:, used_a:, :] = jnp.zeros((nf, n * piece_a - used_a, half), f32)
    cs_a[...] = part_a[other].astype(WIRE)
    mate_a = remote(cs_a, cr_a, c_send.at[0], c_recv.at[0], mate)
    mate_a.start()

    delta1 = (contract(d2[...], w2_ref[...], 1, 1) * slope1[...]).astype(bf16)
    d1[...] = delta1
    grad_b1 = jnp.sum(delta1.astype(f32), axis=0, keepdims=True)

    def span(k, piece):
        return pl.ds(pl.multiple_of(k * piece, piece), piece)

    def scatter_copy(k, piece, src, dst, send, recv):
        target = lax.rem(me + k, n)
        return remote(
            src.at[span(target, piece)], dst.at[k - 1], send.at[k], recv.at[k], peer(k)
        )

    def scatter_a(k):
        return scatter_copy(k, piece_a, rs_a, rr_a, rs_send_a, rs_recv_a)

    def scatter_b(k):
        return scatter_copy(k, piece_b, rs_b, rr_b, rs_send_b, rs_recv_b)

    mate_a.wait()
    chip_a = part_a[core] + cr_a[...].astype(f32)
    part_a[core] = chip_a
    rs_a[...] = chip_a.astype(WIRE)
    each(n, lambda k: scatter_a(k).start())

    grad = contract(hid[...], d1[...], 0, 0)
    for c in range(nf):
        part_b[c, 0:hidden, :] = grad[:, c * half : (c + 1) * half]
    back = contract(d1[...], w1_ref[...], 1, 1).astype(bf16)
    small = jnp.concatenate(
        [
            contract(feat[...], back, 1, 0),
            contract(params_ref[...], back, 1, 0),
            grad_b2,
            grad_b1,
        ],
        axis=0,
    )
    used_b = hidden + levels + n_par + 2
    fill = jnp.zeros((nf, n * piece_b - used_b, half), f32)
    for c in range(nf):
        part_b[c, hidden:used_b, :] = small[:, c * half : (c + 1) * half]
    part_b[:, used_b:, :] = fill
    cs_b[...] = part_b[other].astype(WIRE)
    mate_b = remote(cs_b, cr_b, c_send.at[1], c_recv.at[1], mate)
    mate_b.start()
    gc_ref[...] = contract(proj_ref[...], back, 1, 1)

    mate_b.wait()
    chip_b = part_b[core] + cr_b[...].astype(f32)
    part_b[core] = chip_b
    rs_b[...] = chip_b.astype(WIRE)
    each(n, lambda k: scatter_b(k).start())

    def own_sum(piece, part, received, gathered):
        total = part[core, span(me, piece), :]
        if n <= 16:
            for k in range(1, n):
                total = total + received[k - 1].astype(f32)
        else:
            total = lax.fori_loop(
                1, n, lambda k, acc: acc + received[k - 1].astype(f32), total
            )
        gathered[core, span(me, piece), :] = (total * scale).astype(WIRE)

    def gathers(piece, buffer, send, recv, fsend, frecv):
        mine = buffer.at[core, span(me, piece)]

        def out(k):
            return remote(mine, mine, send.at[k], recv.at[k], peer(k))

        def forward(k):
            held = buffer.at[core, span(source(k), piece)]
            return remote(held, held, fsend.at[k], frecv.at[k], mate)

        return out, forward

    out_a, forward_a = gathers(piece_a, ag_a, ag_send_a, ag_recv_a, fw_send_a, fw_recv_a)
    out_b, forward_b = gathers(piece_b, ag_b, ag_send_b, ag_recv_b, fw_send_b, fw_recv_b)

    each(n, lambda k: scatter_a(k).wait())
    own_sum(piece_a, part_a, rr_a, ag_a)
    each(n, lambda k: out_a(k).start())
    forward_a(0).start()
    each(n, lambda k: scatter_b(k).wait())
    own_sum(piece_b, part_b, rr_b, ag_b)
    each(n, lambda k: out_b(k).start())
    forward_b(0).start()

    def pass_on(out, forward):
        def step(k):
            out(k).wait_recv()
            forward(k).start()

        each(n, step)

    pass_on(out_a, forward_a)
    forward_a(0).wait()
    each(n, lambda k: forward_a(k).wait())
    each(n, lambda k: out_a(k).wait_send())
    for c in range(nf):
        go_ref[c * half : (c + 1) * half, :] = ag_a[c, 0:half, :].astype(f32)
        gw2_ref[:, c * half : (c + 1) * half] = ag_a[c, half:used_a, :].astype(f32)

    pass_on(out_b, forward_b)
    forward_b(0).wait()
    each(n, lambda k: forward_b(k).wait())
    each(n, lambda k: out_b(k).wait_send())
    for c in range(nf):
        lanes = slice(c * half, (c + 1) * half)
        gw1_ref[:, lanes] = ag_b[c, 0:hidden, :].astype(f32)
        tail = ag_b[c, hidden:, :].astype(f32)
        gt_ref[:, lanes] = tail[0:levels]
        gp_ref[:, lanes] = tail[levels : levels + n_par]
        gb2_ref[:, lanes] = tail[levels + n_par : levels + n_par + 1]
        gb1_ref[:, lanes] = tail[levels + n_par + 1 : levels + n_par + 2]


def round_up(value, step):
    return -(-value // step) * step


def body(
    adjoint,
    target_x,
    target_y,
    target_z,
    assignment,
    level_codes,
    cell_params,
    level_table,
    w_proj,
    w_one,
    b_one,
    w_two,
    b_two,
    w_out,
):
    n = lax.axis_size("cells")
    nf = lax.axis_size("freq")
    cells = level_codes.shape[0]
    local = target_x.shape[0]
    hidden = w_one.shape[0]
    levels = level_table.shape[0]
    n_par = w_proj.shape[0]
    outs = w_out.shape[1]
    half = hidden // nf
    per = math.gcd(n, max(1, LANES // local))
    piece_a = round_up(-(-(half + hidden) // n), WIRE_ROWS)
    piece_b = round_up(-(-(hidden + levels + n_par + 2) // n), WIRE_ROWS)
    rows_a, rows_b = n * piece_a, n * piece_b
    scale = 1.0 / math.sqrt(cells * n * nf)
    vmem = pl.BlockSpec(memory_space=pltpu.VMEM)
    dma = pltpu.SemaphoreType.DMA
    results = pl.pallas_call(
        functools.partial(kernel, (n, nf, per, piece_a, piece_b, scale)),
        out_shape=[
            jax.ShapeDtypeStruct((hidden, outs), f32),
            jax.ShapeDtypeStruct((hidden, hidden), f32),
            jax.ShapeDtypeStruct((1, hidden), f32),
            jax.ShapeDtypeStruct((hidden, hidden), f32),
            jax.ShapeDtypeStruct((1, hidden), f32),
            jax.ShapeDtypeStruct((levels, hidden), f32),
            jax.ShapeDtypeStruct((n_par, hidden), f32),
            jax.ShapeDtypeStruct((n_par, cells), f32),
        ],
        in_specs=[vmem] * 14,
        out_specs=[vmem] * 8,
        scratch_shapes=[
            pltpu.VMEM((n, 8, per * local), f32),
            pltpu.VMEM((levels, cells), bf16),
            pltpu.VMEM((cells, hidden), bf16),
            pltpu.VMEM((cells, hidden), bf16),
            pltpu.VMEM((cells, hidden), f32),
            pltpu.VMEM((cells, hidden), bf16),
            pltpu.VMEM((cells, hidden), f32),
            pltpu.VMEM((cells, outs), bf16),
            pltpu.VMEM((cells, hidden), bf16),
            pltpu.VMEM((cells, hidden), bf16),
            pltpu.VMEM((nf, rows_a, half), f32),
            pltpu.VMEM((nf, rows_b, half), f32),
            pltpu.VMEM((rows_a, half), WIRE),
            pltpu.VMEM((rows_b, half), WIRE),
            pltpu.VMEM((rows_a, half), WIRE),
            pltpu.VMEM((rows_b, half), WIRE),
            pltpu.VMEM((rows_a, half), WIRE),
            pltpu.VMEM((rows_b, half), WIRE),
            pltpu.VMEM((n - 1, piece_a, half), WIRE),
            pltpu.VMEM((n - 1, piece_b, half), WIRE),
            pltpu.VMEM((nf, rows_a, half), WIRE),
            pltpu.VMEM((nf, rows_b, half), WIRE),
            dma((n,)),
            dma((n,)),
            dma((2,)),
            dma((2,)),
        ]
        + [dma((n,))] * 12,
        compiler_params=pltpu.CompilerParams(collective_id=0, has_side_effects=True),
        name="hologram_adjoint",
    )(
        adjoint,
        target_x[None, :],
        target_y[None, :],
        target_z[None, :],
        assignment[None, :],
        level_codes[None, :],
        cell_params,
        level_table,
        w_proj,
        w_one,
        b_one[None, :],
        w_two,
        b_two[None, :],
        w_out,
    )
    grad_out, grad_w2, grad_b2, grad_w1, grad_b1, grad_table, grad_proj, grad_params = results
    return (
        grad_out,
        grad_w2,
        grad_b2[0],
        grad_w1,
        grad_b1[0],
        grad_table,
        grad_proj,
        grad_params,
    )


def solution(mesh):
    placed = (
        P(None, ("groups", "cells")),
        P(("groups", "cells")),
        P(("groups", "cells")),
        P(("groups", "cells")),
        P(("groups", "cells")),
        P(("groups", "cells", "freq")),
        P(None, ("groups", "cells", "freq")),
        P(),
        P(),
        P(),
        P(),
        P(),
        P(),
        P(),
    )
    return jax.shard_map(
        body,
        mesh=mesh,
        in_specs=placed,
        out_specs=(
            P("groups", None),
            P("groups", None),
            P("groups"),
            P("groups", None),
            P("groups"),
            P("groups", None),
            P("groups", None),
            P(None, ("groups", "cells", "freq")),
        ),
        check_vma=False,
    )
```

```python
import functools
import math

import jax
import jax.numpy as jnp
from jax import lax
from jax.experimental import pallas as pl
from jax.experimental.pallas import tpu as pltpu
from jax.sharding import PartitionSpec as P

SIDE = 1024
LANES = 128
WIRE = jnp.bfloat16
WIRE_ROWS = 8
VMEM_GRANT = 25165824

wave_low = 1.0
wave_high = 3.0
kernel_gain = 150.0

f32 = jnp.float32
bf16 = jnp.bfloat16


def contract(left, right, left_dim, right_dim):
    return lax.dot_general(
        left, right, (((left_dim,), (right_dim,)), ((), ())), preferred_element_type=f32
    )


def sin_cos(phase):
    turns = jnp.floor(phase * (2.0 / math.pi) + 0.5)
    rest = phase - turns * 1.5703125
    rest = rest - turns * 4.837512969970703125e-4
    rest = rest - turns * 7.54978995489188216e-8
    square = rest * rest
    sine = rest + rest * square * (
        -1.6666654611e-1 + square * (8.3321608736e-3 + square * -1.9515295891e-4)
    )
    cosine = (
        1.0
        - 0.5 * square
        + square
        * square
        * (4.166664568298827e-2 + square * (-1.388731625493765e-3 + square * 2.443315711809948e-5))
    )
    quarter = turns.astype(jnp.int32)
    odd = (quarter & 1) == 1
    sin_part = jnp.where(odd, cosine, sine)
    cos_part = jnp.where(odd, sine, cosine)
    sin_part = jnp.where((quarter & 2) == 2, -sin_part, sin_part)
    cos_part = jnp.where(((quarter + 1) & 2) == 2, -cos_part, cos_part)
    return sin_part, cos_part


def each(count, step):
    if count <= 16:
        for k in range(1, count):
            step(k)
    else:

        @pl.loop(1, count)
        def _(k):
            step(k)


def kernel(
    dims,
    *refs,
):
    inputs, results, loaded = refs[:14], refs[14:17], refs[17:31]
    refs = results + refs[31:]
    (
        ag_a,
        ag_b,
        gc_ref,
        gath,
        feat,
        hid,
        act1,
        slope1,
        act2,
        slope2,
        spec,
        d2,
        d1,
        part_a,
        part_b,
        cs_a,
        cs_b,
        cr_a,
        cr_b,
        rs_a,
        rs_b,
        rr_a,
        rr_b,
        g_send,
        g_recv,
        c_send,
        c_recv,
        rs_send_a,
        rs_recv_a,
        rs_send_b,
        rs_recv_b,
        ag_send_a,
        ag_recv_a,
        ag_send_b,
        ag_recv_b,
        fw_send_a,
        fw_recv_a,
        fw_send_b,
        fw_recv_b,
        load_sem,
    ) = refs
    (
        adj_ref,
        x_ref,
        y_ref,
        z_ref,
        asg_ref,
        codes_ref,
        params_ref,
        table_ref,
        proj_ref,
        w1_ref,
        b1_ref,
        w2_ref,
        b2_ref,
        wo_ref,
    ) = loaded
    n, nf, per, piece_a, piece_b, scale = dims
    me = lax.axis_index("cells")
    core = lax.axis_index("freq")
    other = 1 - core
    cells = codes_ref.shape[1]
    local = x_ref.shape[1]
    hidden = w1_ref.shape[0]
    half = hidden // nf
    levels = table_ref.shape[0]
    n_par = proj_ref.shape[0]
    outs = wo_ref.shape[1]
    freqs = outs // 2

    def peer(k):
        return {"cells": lax.rem(me + k, n)}

    def source(k):
        return lax.rem(me + n - k, n)

    mate = {"freq": other}

    def remote(src, dst, send, recv, device):
        return pltpu.make_async_remote_copy(
            src_ref=src,
            dst_ref=dst,
            send_sem=send,
            recv_sem=recv,
            device_id=device,
            device_id_type=pl.DeviceIdType.MESH,
        )

    barrier = pltpu.get_barrier_semaphore()
    each(
        n,
        lambda k: pl.semaphore_signal(
            barrier, inc=1, device_id=peer(k), device_id_type=pl.DeviceIdType.MESH
        ),
    )
    pl.semaphore_signal(barrier, inc=1, device_id=mate, device_id_type=pl.DeviceIdType.MESH)

    loads = [
        pltpu.make_async_copy(src, dst, load_sem.at[i])
        for i, (src, dst) in enumerate(zip(inputs, loaded))
    ]
    for load in loads:
        load.start()
    for load in loads[:5]:
        load.wait()

    width = per * local
    rows = jnp.concatenate(
        [
            adj_ref[...],
            x_ref[...],
            y_ref[...],
            z_ref[...],
            asg_ref[...].astype(f32),
            jnp.zeros((2, local), f32),
        ],
        axis=0,
    )
    spread = jnp.concatenate([rows] * per, axis=1)
    lane = lax.broadcasted_iota(jnp.int32, (8, width), 1)
    start = lax.rem(me, per) * local
    inside = jnp.logical_and(lane >= start, lane < start + local)
    gath[me] = jnp.where(inside, spread, 0.0)

    for load in loads[5:11]:
        load.wait()
    codes = codes_ref[...]
    onehot = (
        jnp.where(codes == lax.broadcasted_iota(jnp.int32, (levels, cells), 0), 1.0, 0.0)
    ).astype(bf16)
    feat[0:levels, :] = onehot
    hid[...] = (
        contract(onehot, table_ref[...], 0, 0) + contract(params_ref[...], proj_ref[...], 0, 0)
    ).astype(bf16)
    pre = contract(hid[...], w1_ref[...], 1, 0) + b1_ref[...]
    sig = 1.0 / (1.0 + jnp.exp(-pre))
    act1[...] = (pre * sig).astype(bf16)
    slope1[...] = sig * (1.0 + pre * (1.0 - sig))

    pl.semaphore_wait(barrier, n)

    def gather_copy(k):
        return remote(gath.at[me], gath.at[me], g_send.at[k], g_recv.at[k], peer(k))

    each(n, lambda k: gather_copy(k).start())

    for load in loads[11:]:
        load.wait()
    pre = contract(act1[...], w2_ref[...], 1, 0) + b2_ref[...]
    sig = 1.0 / (1.0 + jnp.exp(-pre))
    act2[...] = (pre * sig).astype(bf16)
    slope2[...] = sig * (1.0 + pre * (1.0 - sig))

    each(n, lambda k: gather_copy(k).wait())

    index = (me * nf + core) * cells + lax.broadcasted_iota(jnp.int32, (cells, width), 0)
    cell_col = (index % SIDE).astype(f32)
    cell_row = (index // SIDE).astype(f32)
    line = lax.broadcasted_iota(jnp.int32, (outs, width), 0)
    upper = line < freqs
    freq_line = jnp.where(upper, line, line - freqs).astype(f32)

    def section(first):
        block = gath[first]
        for j in range(1, per):
            block = block + gath[first + j]
        adj = block[0:2].astype(bf16).astype(f32)
        a0, a1 = adj[0:1], adj[1:2]
        px, py, pz, pf = block[2:3], block[3:4], block[4:5], block[5:6]
        wave = wave_low + (wave_high - wave_low) * pf / (freqs - 1)
        off_x = px - cell_col
        off_y = py - cell_row
        square = off_x * off_x + off_y * off_y + pz * pz
        distance = jnp.sqrt(square)
        amplitude = (kernel_gain * pz) / square
        sine, cosine = sin_cos(wave * distance)
        kre = (amplitude * cosine).astype(bf16)
        kim = (amplitude * sine).astype(bf16)
        chosen = freq_line == pf
        left_re = jnp.where(chosen, jnp.where(upper, a0, a1), 0.0).astype(bf16)
        left_im = jnp.where(chosen, jnp.where(upper, a1, -a0), 0.0).astype(bf16)
        return contract(kre, left_re, 1, 1) + contract(kim, left_im, 1, 1)

    if n == per:
        total = section(0)
    else:
        total = lax.fori_loop(
            0,
            n // per,
            lambda i, acc: acc + section(i * per),
            jnp.zeros((cells, outs), f32),
        )
    spec[...] = total.astype(bf16)

    delta2 = (contract(spec[...], wo_ref[...], 1, 1) * slope2[...]).astype(bf16)
    d2[...] = delta2
    grad_b2 = jnp.sum(delta2.astype(f32), axis=0, keepdims=True)
    grad = contract(act2[...], spec[...], 0, 0)
    for c in range(nf):
        part_a[c, 0:half, :] = grad[c * half : (c + 1) * half]
    grad = contract(act1[...], d2[...], 0, 0)
    for c in range(nf):
        part_a[c, half : half + hidden, :] = grad[:, c * half : (c + 1) * half]
    used_a = half + hidden
    if used_a < n * piece_a:
        part_a[:, used_a:, :] = jnp.zeros((nf, n * piece_a - used_a, half), f32)
    cs_a[...] = part_a[other].astype(WIRE)
    mate_a = remote(cs_a, cr_a, c_send.at[0], c_recv.at[0], mate)
    mate_a.start()

    delta1 = (contract(d2[...], w2_ref[...], 1, 1) * slope1[...]).astype(bf16)
    d1[...] = delta1
    grad_b1 = jnp.sum(delta1.astype(f32), axis=0, keepdims=True)

    def span(k, piece):
        return pl.ds(pl.multiple_of(k * piece, piece), piece)

    def scatter_copy(k, piece, src, dst, send, recv):
        target = lax.rem(me + k, n)
        return remote(
            src.at[span(target, piece)], dst.at[k - 1], send.at[k], recv.at[k], peer(k)
        )

    def scatter_a(k):
        return scatter_copy(k, piece_a, rs_a, rr_a, rs_send_a, rs_recv_a)

    def scatter_b(k):
        return scatter_copy(k, piece_b, rs_b, rr_b, rs_send_b, rs_recv_b)

    mate_a.wait()
    chip_a = part_a[core] + cr_a[...].astype(f32)
    part_a[core] = chip_a
    rs_a[...] = chip_a.astype(WIRE)
    each(n, lambda k: scatter_a(k).start())

    grad = contract(hid[...], d1[...], 0, 0)
    for c in range(nf):
        part_b[c, 0:hidden, :] = grad[:, c * half : (c + 1) * half]
    back = contract(d1[...], w1_ref[...], 1, 1).astype(bf16)
    small = jnp.concatenate(
        [
            contract(feat[...], back, 1, 0),
            contract(params_ref[...], back, 1, 0),
            grad_b2,
            grad_b1,
        ],
        axis=0,
    )
    used_b = hidden + levels + n_par + 2
    fill = jnp.zeros((nf, n * piece_b - used_b, half), f32)
    for c in range(nf):
        part_b[c, hidden:used_b, :] = small[:, c * half : (c + 1) * half]
    part_b[:, used_b:, :] = fill
    cs_b[...] = part_b[other].astype(WIRE)
    mate_b = remote(cs_b, cr_b, c_send.at[1], c_recv.at[1], mate)
    mate_b.start()
    gc_ref[...] = contract(proj_ref[...], back, 1, 1)

    mate_b.wait()
    chip_b = part_b[core] + cr_b[...].astype(f32)
    part_b[core] = chip_b
    rs_b[...] = chip_b.astype(WIRE)
    each(n, lambda k: scatter_b(k).start())

    def own_sum(piece, part, received, gathered):
        total = part[core, span(me, piece), :]
        if n <= 16:
            for k in range(1, n):
                total = total + received[k - 1].astype(f32)
        else:
            total = lax.fori_loop(
                1, n, lambda k, acc: acc + received[k - 1].astype(f32), total
            )
        gathered[core, span(me, piece), :] = (total * scale).astype(WIRE)

    def gathers(piece, buffer, send, recv, fsend, frecv):
        mine = buffer.at[core, span(me, piece)]

        def out(k):
            return remote(mine, mine, send.at[k], recv.at[k], peer(k))

        def forward(k):
            held = buffer.at[core, span(source(k), piece)]
            return remote(held, held, fsend.at[k], frecv.at[k], mate)

        return out, forward

    out_a, forward_a = gathers(piece_a, ag_a, ag_send_a, ag_recv_a, fw_send_a, fw_recv_a)
    out_b, forward_b = gathers(piece_b, ag_b, ag_send_b, ag_recv_b, fw_send_b, fw_recv_b)

    each(n, lambda k: scatter_a(k).wait())
    own_sum(piece_a, part_a, rr_a, ag_a)
    each(n, lambda k: out_a(k).start())
    forward_a(0).start()
    each(n, lambda k: scatter_b(k).wait())
    own_sum(piece_b, part_b, rr_b, ag_b)
    each(n, lambda k: out_b(k).start())
    forward_b(0).start()

    def pass_on(out, forward):
        def step(k):
            out(k).wait_recv()
            forward(k).start()

        each(n, step)

    pass_on(out_a, forward_a)
    forward_a(0).wait()
    each(n, lambda k: forward_a(k).wait())
    each(n, lambda k: out_a(k).wait_send())

    pass_on(out_b, forward_b)
    forward_b(0).wait()
    each(n, lambda k: forward_b(k).wait())
    each(n, lambda k: out_b(k).wait_send())

def unpack(
    ag_a,
    ag_b,
    gc_in,
    go_ref,
    gw2_ref,
    gb2_ref,
    gw1_ref,
    gb1_ref,
    gt_ref,
    gp_ref,
    gc_ref,
):
    nf, _, half = ag_a.shape
    hidden = gw2_ref.shape[0]
    levels, n_par = gt_ref.shape[0], gp_ref.shape[0]
    for c in range(nf):
        lanes = slice(c * half, (c + 1) * half)
        go_ref[lanes, :] = ag_a[c, 0:half, :].astype(f32)
        gw2_ref[:, lanes] = ag_a[c, half : half + hidden, :].astype(f32)
        gw1_ref[:, lanes] = ag_b[c, 0:hidden, :].astype(f32)
        tail = ag_b[c, hidden:, :].astype(f32)
        gt_ref[:, lanes] = tail[0:levels]
        gp_ref[:, lanes] = tail[levels : levels + n_par]
        gb2_ref[:, lanes] = tail[levels + n_par : levels + n_par + 1]
        gb1_ref[:, lanes] = tail[levels + n_par + 1 : levels + n_par + 2]
    gc_ref[...] = gc_in[...]


def round_up(value, step):
    return -(-value // step) * step


def body(
    adjoint,
    target_x,
    target_y,
    target_z,
    assignment,
    level_codes,
    cell_params,
    level_table,
    w_proj,
    w_one,
    b_one,
    w_two,
    b_two,
    w_out,
):
    n = lax.axis_size("cells")
    nf = lax.axis_size("freq")
    cells = level_codes.shape[0]
    local = target_x.shape[0]
    hidden = w_one.shape[0]
    levels = level_table.shape[0]
    n_par = w_proj.shape[0]
    outs = w_out.shape[1]
    half = hidden // nf
    per = math.gcd(n, max(1, LANES // local))
    piece_a = round_up(-(-(half + hidden) // n), WIRE_ROWS)
    piece_b = round_up(-(-(hidden + levels + n_par + 2) // n), WIRE_ROWS)
    rows_a, rows_b = n * piece_a, n * piece_b
    scale = 1.0 / math.sqrt(cells * n * nf)
    vmem = pl.BlockSpec(memory_space=pltpu.VMEM)
    dma = pltpu.SemaphoreType.DMA
    args = (
        adjoint,
        target_x[None, :],
        target_y[None, :],
        target_z[None, :],
        assignment[None, :],
        level_codes[None, :],
        cell_params,
        level_table,
        w_proj,
        w_one,
        b_one[None, :],
        w_two,
        b_two[None, :],
        w_out,
    )
    packed = pl.pallas_call(
        functools.partial(kernel, (n, nf, per, piece_a, piece_b, scale)),
        out_shape=[
            pltpu.VMEM((nf, rows_a, half), WIRE),
            pltpu.VMEM((nf, rows_b, half), WIRE),
            pltpu.VMEM((n_par, cells), f32),
        ],
        in_specs=[pl.BlockSpec(memory_space=pltpu.HBM)] * 14,
        out_specs=[vmem] * 3,
        scratch_shapes=[pltpu.VMEM(arg.shape, arg.dtype) for arg in args]
        + [
            pltpu.VMEM((n, 8, per * local), f32),
            pltpu.VMEM((levels, cells), bf16),
            pltpu.VMEM((cells, hidden), bf16),
            pltpu.VMEM((cells, hidden), bf16),
            pltpu.VMEM((cells, hidden), f32),
            pltpu.VMEM((cells, hidden), bf16),
            pltpu.VMEM((cells, hidden), f32),
            pltpu.VMEM((cells, outs), bf16),
            pltpu.VMEM((cells, hidden), bf16),
            pltpu.VMEM((cells, hidden), bf16),
            pltpu.VMEM((nf, rows_a, half), f32),
            pltpu.VMEM((nf, rows_b, half), f32),
            pltpu.VMEM((rows_a, half), WIRE),
            pltpu.VMEM((rows_b, half), WIRE),
            pltpu.VMEM((rows_a, half), WIRE),
            pltpu.VMEM((rows_b, half), WIRE),
            pltpu.VMEM((rows_a, half), WIRE),
            pltpu.VMEM((rows_b, half), WIRE),
            pltpu.VMEM((n - 1, piece_a, half), WIRE),
            pltpu.VMEM((n - 1, piece_b, half), WIRE),
            dma((n,)),
            dma((n,)),
            dma((2,)),
            dma((2,)),
        ]
        + [dma((n,))] * 12
        + [dma((len(args),))],
        compiler_params=pltpu.CompilerParams(
            collective_id=0, has_side_effects=True, vmem_limit_bytes=VMEM_GRANT
        ),
        name="hologram_adjoint",
    )(*[pltpu.with_memory_space_constraint(arg, pltpu.HBM) for arg in args])
    results = pl.pallas_call(
        unpack,
        out_shape=[
            jax.ShapeDtypeStruct((hidden, outs), f32),
            jax.ShapeDtypeStruct((hidden, hidden), f32),
            jax.ShapeDtypeStruct((1, hidden), f32),
            jax.ShapeDtypeStruct((hidden, hidden), f32),
            jax.ShapeDtypeStruct((1, hidden), f32),
            jax.ShapeDtypeStruct((levels, hidden), f32),
            jax.ShapeDtypeStruct((n_par, hidden), f32),
            jax.ShapeDtypeStruct((n_par, cells), f32),
        ],
        in_specs=[vmem] * 3,
        out_specs=[vmem] * 8,
        compiler_params=pltpu.CompilerParams(vmem_limit_bytes=VMEM_GRANT),
        name="unpack",
    )(*packed)
    grad_out, grad_w2, grad_b2, grad_w1, grad_b1, grad_table, grad_proj, grad_params = results
    return (
        grad_out,
        grad_w2,
        grad_b2[0],
        grad_w1,
        grad_b1[0],
        grad_table,
        grad_proj,
        grad_params,
    )


def solution(mesh):
    placed = (
        P(None, ("groups", "cells")),
        P(("groups", "cells")),
        P(("groups", "cells")),
        P(("groups", "cells")),
        P(("groups", "cells")),
        P(("groups", "cells", "freq")),
        P(None, ("groups", "cells", "freq")),
        P(),
        P(),
        P(),
        P(),
        P(),
        P(),
        P(),
    )
    return jax.shard_map(
        body,
        mesh=mesh,
        in_specs=placed,
        out_specs=(
            P("groups", None),
            P("groups", None),
            P("groups"),
            P("groups", None),
            P("groups"),
            P("groups", None),
            P("groups", None),
            P(None, ("groups", "cells", "freq")),
        ),
        check_vma=False,
    )
```
